32 devices in a mesh: segment: 4 (over y, x), lane: 8 (over z, core).
Axes of the slice: x: 2, y: 2, z: 4, core: 2. Of those that a mesh axis runs over, the one named last changes fastest.
Arguments:
- spectra: float32 [4, 4096, 1024], P(None, 'lane'), may hold values from -6 to 6
- rfi_flags: int32 [4, 4096, 8], P(None, 'lane'), may hold values 0 or 1
- sub_delay: int32 [64, 4096], P(None, 'lane'), may hold values from 0 to 7
- fine_delay: int32 [2048, 64], P('lane'), may hold values from 0 to 31
- widths: int32 [8], replicated, may hold values from 1 to 64
Outputs:
- peaks: float32 [4, 2048, 8], P('segment', 'lane')
The draws below stay inside these ranges and needn't reach their ends.
All inputs are finite; a program needn't handle non-finite values. No bound on the sum of `rfi_flags` on one device may be relied on, other than what follows from the above.
Results may differ from the reference program's by a relative error of at most 0.0001.
Values sent between devices are 32-bit elements; how exact they have to be, the bound alone decides.
A program may use at most 128 MiB of HBM per device.

```python
import jax
import jax.numpy as jnp
from jax import lax

C = 4096
SUBCH = 64
NSUB = 64
NCOARSE = 64
NDM = 2048
S = 1024
M = 4
BLK = 128
D1 = 8
D2 = 32
NW = 8
WMAX = 64


def touch_ends(array, stream_key, low, largest):
    place = [jax.random.randint(jax.random.fold_in(stream_key, axis), (), 0, length) for axis, length in enumerate(array.shape)]
    widest = array.shape.index(max(array.shape))
    neighbour = place[:widest] + [(place[widest] + 1) % array.shape[widest]] + place[widest + 1:]
    return array.at[tuple(place)].set(low).at[tuple(neighbour)].set(largest)


def levels(key, extent, shards, least, largest):
    factor_of = 1.0
    for position, parts in shards:
        draws = jax.random.uniform(jax.random.fold_in(jax.random.fold_in(key, 6), position), (parts,), jnp.float32, least / len(shards), largest / len(shards))
        factor_of = factor_of * jnp.repeat(jnp.exp(draws), extent[position] // parts).reshape((-1,) + (1,) * (len(extent) - 1 - position))
    return factor_of


def bell_draw(stream_key, extent, scale, most, split=(), kind=jnp.bfloat16):
    loudness = levels(stream_key, extent, split, -0.22, 0.18) if split else 1.0
    drawn = jax.random.normal(stream_key, extent, jnp.float32) * scale * loudness
    return jnp.minimum(jnp.maximum(drawn, -most), most).astype(kind)


def setup_inputs(seed: int = 0) -> dict:
    arg_keys = jax.random.split(jax.random.key(seed), 6)
    return {
        "spectra": bell_draw(arg_keys[0], (M, C, S), 1.0, 6.0, ((1, 8),), jnp.float32),
        "rfi_flags": touch_ends((jax.random.randint(arg_keys[1], (M, C, S // BLK), 0, 8) < 1).astype(jnp.int32), jax.random.fold_in(arg_keys[1], 1), 0, 1),
        "sub_delay": touch_ends(jax.random.randint(arg_keys[2], (NCOARSE, C), 0, D1), jax.random.fold_in(arg_keys[2], 1), 0, D1 - 1).astype(jnp.int32),
        "fine_delay": touch_ends(jax.random.randint(arg_keys[3], (NDM, NSUB), 0, D2), jax.random.fold_in(arg_keys[3], 1), 0, D2 - 1).astype(jnp.int32),
        "widths": touch_ends(jax.random.randint(arg_keys[4], (NW,), 1, WMAX + 1), jax.random.fold_in(arg_keys[4], 1), 1, WMAX).astype(jnp.int32),
    }


def clean_block(power_in, flag_rows, block_len):
    row_count, samples = power_in.shape
    kept_mask = 1.0 - flag_rows.astype(jnp.float32)
    kept_mask = jnp.broadcast_to(kept_mask[:, :, None], (row_count, flag_rows.shape[1], block_len)).reshape(row_count, samples)
    masked = kept_mask * power_in
    centre = lax.optimization_barrier(jnp.mean(masked, axis=1, keepdims=True))
    spread = lax.optimization_barrier(jnp.mean((masked - centre) * (masked - centre), axis=1, keepdims=True))
    return kept_mask * (power_in - centre) * lax.rsqrt(spread + 1e-05)

def detect(centered, widths, total_sq, cell_count):
    sigma = jnp.sqrt(total_sq / cell_count + 1e-06)
    samples = centered.shape[1]
    prefix = jnp.concatenate([jnp.zeros((centered.shape[0], 1), jnp.float32), jnp.cumsum(centered, axis=1)], axis=1)
    sample_idx = jnp.arange(samples, dtype=jnp.int32)
    ends = jnp.minimum(sample_idx[None, :] + widths[:, None], samples)
    upper = prefix[:, ends]
    lower = prefix[:, None, :samples]
    scaled = (upper - lower) / (sigma * jnp.sqrt(widths.astype(jnp.float32)))[None, :, None]
    return lax.optimization_barrier(jnp.max(scaled, axis=2))

def reference(spectra, rfi_flags, sub_delay, fine_delay, widths):
    sample_idx = jnp.arange(S, dtype=jnp.int32)
    owners = jnp.arange(NDM, dtype=jnp.int32) // (NDM // NCOARSE)
    outputs = []
    for batch in range(M):
        normed = clean_block(spectra[batch], rfi_flags[batch], BLK)
        zero_level = lax.optimization_barrier(jnp.sum(normed, axis=0)) / C
        cleaned = normed - zero_level[None, :]
        padded = jnp.pad(cleaned, ((0, 0), (0, D1)))

        def coarse_row(delay_row):
            lookup = sample_idx[None, :] + delay_row[:, None]
            picked = jnp.take_along_axis(padded, lookup, axis=1)
            return picked.reshape(NSUB, SUBCH, S).sum(axis=1)
        subbands = lax.map(coarse_row, sub_delay)
        sub_padded = jnp.pad(subbands, ((0, 0), (0, 0), (0, D2)))

        def dm_row(entry_pair):
            delay_row, owner_row = entry_pair
            source = lax.dynamic_index_in_dim(sub_padded, owner_row, 0, keepdims=False)
            lookup = sample_idx[None, :] + delay_row[:, None]
            return jnp.take_along_axis(source, lookup, axis=1).sum(axis=0)
        series = lax.map(dm_row, (fine_delay, owners))
        centered = series - lax.optimization_barrier(jnp.mean(series, axis=1, keepdims=True))
        total_sq = jnp.sum(centered * centered)
        outputs.append(detect(centered, widths, total_sq, NDM * S))
    return jnp.stack(outputs)
```

```python
import functools

import jax
import jax.numpy as jnp
from jax import lax
from jax.experimental import pallas as pl
from jax.experimental.pallas import tpu as pltpu
from jax.sharding import PartitionSpec as P

D1 = 8
D2 = 32
LANES = 128

F32 = jnp.float32
BF16 = jnp.bfloat16


def iota(shape, axis):
    return lax.broadcasted_iota(jnp.int32, shape, axis)


def split(x):
    hi = x.astype(BF16)
    lo = (x - hi.astype(F32)).astype(BF16)
    return hi, lo


def dot(a, b):
    return lax.dot_general(a, b, (((1,), (0,)), ((), ())), preferred_element_type=F32)


def hot(mask):
    return jnp.where(mask, 1.0, 0.0).astype(BF16)


def shift_lanes(x, by):
    if by == 0:
        return x
    rolled = pltpu.roll(x, LANES - by, 1)
    return jnp.where(iota(x.shape, 1) < LANES - by, rolled, 0.0)


def search_kernel(
    cfg,
    spectra,
    flags,
    sub_delay,
    fine_delay,
    centered_ref,
    total_ref,
    power,
    flag_rows,
    normed,
    perm,
    delays2,
    wc,
    xs,
    out_blocks,
    incoming,
    fine_rep,
    wf,
    zmine,
    zall,
    smine,
    sall,
    in_sems,
    own_sems,
    send_sems,
    recv_sems,
    zsend,
    zrecv,
    ssend,
    srecv,
):
    lanes, R, NB, SUB, CD, NH, QC, QF, NSUB, PER = cfg
    KC = CD // NH
    samples = R * LANES
    rows = NB * SUB
    me = lax.axis_index("lane")
    batch = lax.axis_index("segment")

    load_power = pltpu.make_async_copy(spectra.at[batch], power, in_sems.at[0])
    load_flags = pltpu.make_async_copy(flags.at[batch], flag_rows, in_sems.at[1])
    load_power.start()
    load_flags.start()

    def peer(step):
        return lax.rem(me + step, lanes)

    barrier = pltpu.get_barrier_semaphore()
    for step in range(1, lanes):
        pl.semaphore_signal(barrier, inc=1, device_id={"lane": peer(step)}, device_id_type=pl.DeviceIdType.MESH)

    for r in range(R):
        src = R * iota((samples, LANES), 1) + r
        perm[:, r * LANES : (r + 1) * LANES] = hot(iota((samples, LANES), 0) == src)

    load_power.wait()
    load_flags.wait()

    blocks = flag_rows.shape[1]
    width = samples // blocks
    row_step = min(64, rows)

    def clean(g, _):
        sl = pl.ds(pl.multiple_of(g * row_step, row_step), row_step)
        kept = 1.0 - flag_rows[sl, :].astype(F32)
        mask = jnp.concatenate(
            [jnp.broadcast_to(kept[:, n : n + 1], (row_step, width)) for n in range(blocks)], axis=1
        )
        x = power[sl, :]
        masked = mask * x
        centre = jnp.sum(masked, axis=1, keepdims=True) * (1.0 / samples)
        off = masked - centre
        spread = jnp.sum(off * off, axis=1, keepdims=True) * (1.0 / samples)
        out = mask * (x - centre) * lax.rsqrt(spread + 1e-05)
        hi, lo = split(out)
        both = dot(jnp.concatenate([hi, lo], axis=0), perm[...])
        normed[sl, :] = both[:row_step] + both[row_step:]
        return _

    lax.fori_loop(0, rows // row_step, clean, 0)

    for r in range(R):
        zmine[r : r + 1, :] = jnp.sum(normed[:, r * LANES : (r + 1) * LANES], axis=0, keepdims=True)
    zall[me] = zmine[...]
    pl.semaphore_wait(barrier, lanes - 1)

    def z_copy(step):
        return pltpu.make_async_remote_copy(
            zmine, zall.at[me], zsend.at[step], zrecv.at[step],
            device_id={"lane": peer(step)}, device_id_type=pl.DeviceIdType.MESH,
        )

    for step in range(1, lanes):
        z_copy(step).start()

    per_tile = LANES // SUB
    for b in range(NB):
        block = sub_delay[:, b * SUB : (b + 1) * SUB]
        delays2[b] = jnp.concatenate([block] * per_tile, axis=1)

    def coarse_weights(b, _):
        d = delays2[b]
        d = jnp.broadcast_to(d[:, None, :], (lanes * CD, R, LANES)).reshape(lanes, NH, KC, R, LANES)
        for h in range(NH):
            part = d[:, h].reshape(lanes * KC, R, LANES)
            for q in range(QC):
                for lt in range(R * SUB // LANES):
                    lag = R * q + lt * per_tile + iota((R, LANES), 1) // SUB - iota((R, LANES), 0)
                    n = lanes * KC * R
                    wc[b, h, q * n : (q + 1) * n, lt * LANES : (lt + 1) * LANES] = hot(part == lag[None]).reshape(n, LANES)
        return _

    lax.fori_loop(0, NB, coarse_weights, 0)

    for step in range(1, lanes):
        z_copy(step).wait()
    zero = zall[0]
    for e in range(1, lanes):
        zero = zero + zall[e]
    zmean = zero * (1.0 / (lanes * rows))

    def prepare(b, _):
        sl = pl.ds(pl.multiple_of(b * SUB, SUB), SUB)
        for r in range(R):
            part = normed[sl, r * LANES : (r + 1) * LANES] - zmean[r : r + 1, :]
            hi, lo = split(part)
            xs[b, r * SUB : (r + 1) * SUB, :LANES] = hi
            xs[b, r * SUB : (r + 1) * SUB, LANES:] = lo
        return _

    lax.fori_loop(0, NB, prepare, 0)

    def block_copy(step, h):
        e = peer(step)
        return pltpu.make_async_remote_copy(
            out_blocks.at[h, e],
            incoming.at[h, :, pl.ds(me * NB, NB)],
            send_sems.at[step, h],
            recv_sems.at[step, h],
            device_id={"lane": e},
            device_id_type=pl.DeviceIdType.MESH,
        )

    def own_copy(h):
        return pltpu.make_async_copy(
            out_blocks.at[h, me], incoming.at[h, :, pl.ds(me * NB, NB)], own_sems.at[h]
        )

    for h in range(NH):

        def coarse(b, _):
            n = lanes * KC * R
            o = dot(wc[b, h], xs[b])
            o = o[:, :LANES] + o[:, LANES:]
            total = o[:n]
            for q in range(1, QC):
                total = total + shift_lanes(o[q * n : (q + 1) * n], q)
            out_blocks[h, :, :, b] = total.reshape(lanes, KC, R, LANES)
            return _

        lax.fori_loop(0, NB, coarse, 0)
        for step in range(1, lanes):
            block_copy(step, h).start()
        own_copy(h).start()

    cols = NSUB * R
    rep = hot(iota((NSUB, cols), 1) // R == iota((NSUB, cols), 0))
    fine_rep[...] = dot(fine_delay[...].astype(F32).astype(BF16), rep).astype(jnp.int32)

    def fine_weights(k, _):
        sl = pl.ds(pl.multiple_of(k * PER, PER), PER)
        for lt in range(cols // LANES):
            d = fine_rep[sl, lt * LANES : (lt + 1) * LANES]
            d = jnp.broadcast_to(d[:, None, :], (PER, R, LANES))
            for q in range(QF):
                lag = R * q + iota((R, LANES), 1) % R - iota((R, LANES), 0)
                n = PER * R
                wf[k, q * n : (q + 1) * n, lt * LANES : (lt + 1) * LANES] = hot(d == lag[None]).reshape(n, LANES)
        return _

    lax.fori_loop(0, CD, fine_weights, 0)

    smine[...] = jnp.zeros_like(smine)
    for h in range(NH):
        own_copy(h).wait()
        for step in range(1, lanes):
            block_copy(step, h).wait_recv()

        def fine(kl, _):
            k = h * KC + kl
            n = PER * R
            hi, lo = split(incoming[h, kl].reshape(NSUB * R, LANES))
            o = dot(wf[k], jnp.concatenate([hi, lo], axis=1))
            o = o[:, :LANES] + o[:, LANES:]
            total = o[:n]
            for q in range(1, QF):
                total = total + shift_lanes(o[q * n : (q + 1) * n], q)
            series = total.reshape(PER, R, LANES)
            mean = jnp.sum(jnp.sum(series, axis=1, keepdims=True), axis=2, keepdims=True) * (1.0 / samples)
            series = series - mean
            centered_ref[pl.ds(k * PER, PER)] = series
            smine[...] += jnp.sum(series * series, axis=0)
            return _

        lax.fori_loop(0, KC, fine, 0)

    sall[me] = smine[...]

    def s_copy(step):
        return pltpu.make_async_remote_copy(
            smine, sall.at[me], ssend.at[step], srecv.at[step],
            device_id={"lane": peer(step)}, device_id_type=pl.DeviceIdType.MESH,
        )

    for step in range(1, lanes):
        s_copy(step).start()
    for h in range(NH):
        for step in range(1, lanes):
            block_copy(step, h).wait_send()
    for step in range(1, lanes):
        s_copy(step).wait()
    total = sall[0]
    for e in range(1, lanes):
        total = total + sall[e]
    total_ref[...] = total


def detect_kernel(count, x_ref, total_ref, widths_ref, wrow_ref, out_ref, best):
    trials, R, L = x_ref.shape
    samples = R * L
    nw = widths_ref.shape[0]
    step = min(32, trials)
    upper_tri = hot(iota((L, L), 0) < iota((L, L), 1))

    def body(g, _):
        sl = pl.ds(pl.multiple_of(g * step, step), step)
        x = x_ref[sl]
        flat = x.reshape(step * R, L)
        hi = flat.astype(BF16)
        rest = flat - hi.astype(F32)
        mid = rest.astype(BF16)
        lo = (rest - mid.astype(F32)).astype(BF16)
        before = dot(hi, upper_tri) + dot(mid, upper_tri) + dot(lo, upper_tri)
        before = jnp.sum(before.reshape(step, R, L), axis=1, keepdims=True)
        sub = iota((step, R, L), 1)
        lane = iota((step, R, L), 2)
        run = x
        hop = 1
        while hop < R:
            run = run + jnp.where(sub >= hop, pltpu.roll(run, hop, 1), 0.0)
            hop *= 2
        prefix = before + run - x
        whole = jnp.sum(jnp.sum(x, axis=1, keepdims=True), axis=2, keepdims=True)
        pos = R * lane + sub
        for wi in range(nw):
            w = widths_ref[wi]
            a = w // R
            b = w - a * R
            y = pltpu.roll(prefix, lax.rem(R - b, R), 1)
            y = pltpu.roll(y.reshape(step * R, L), lax.rem(L - a, L), 1)
            y1 = pltpu.roll(y, L - 1, 1).reshape(step, R, L)
            y = jnp.where(sub + b >= R, y1, y.reshape(step, R, L))
            y = jnp.where(pos + w >= samples, whole, y)
            best[wi, sl, :] = jnp.max(y - prefix, axis=1)
        return _

    lax.fori_loop(0, trials // step, body, 0)
    sigma = jnp.sqrt(jnp.sum(total_ref[...], axis=(0, 1), keepdims=True) * (1.0 / count) + 1e-06)
    out = jnp.zeros((trials, LANES), F32)
    for wi in range(nw):
        top = jnp.max(best[wi], axis=1, keepdims=True)
        out = jnp.where(iota((trials, LANES), 1) == wi, top, out)
    scale = sigma * jnp.sqrt(wrow_ref[...].astype(F32))
    out_ref[0] = out[:, :nw] / scale


def body(lanes, spectra, rfi_flags, sub_delay, fine_delay, widths):
    batches, rows, samples = spectra.shape
    R = samples // LANES
    coarse = sub_delay.shape[0]
    trials, NSUB = fine_delay.shape
    SUB = rows * lanes // NSUB
    NB = rows // SUB
    CD = coarse // lanes
    PER = trials // CD
    NH = min(4, CD)
    KC = CD // NH
    QC = (R - 1 + D1 - 1) // R + 1
    QF = (R - 1 + D2 - 1) // R + 1
    cfg = (lanes, R, NB, SUB, CD, NH, QC, QF, NSUB, PER)
    any_spec = pl.BlockSpec(memory_space=pl.ANY)
    vmem = pl.BlockSpec(memory_space=pltpu.VMEM)
    dma = pltpu.SemaphoreType.DMA
    centered, total = pl.pallas_call(
        functools.partial(search_kernel, cfg),
        out_shape=(
            jax.ShapeDtypeStruct((trials, R, LANES), F32),
            jax.ShapeDtypeStruct((R, LANES), F32),
        ),
        in_specs=[any_spec, any_spec, vmem, vmem],
        out_specs=(vmem, vmem),
        scratch_shapes=[
            pltpu.VMEM((rows, samples), F32),
            pltpu.VMEM((rows, rfi_flags.shape[2]), jnp.int32),
            pltpu.VMEM((rows, samples), F32),
            pltpu.VMEM((samples, samples), BF16),
            pltpu.VMEM((NB, coarse, LANES), jnp.int32),
            pltpu.VMEM((NB, NH, QC * lanes * KC * R, R * SUB), BF16),
            pltpu.VMEM((NB, R * SUB, 2 * LANES), BF16),
            pltpu.VMEM((NH, lanes, KC, NB, R, LANES), F32),
            pltpu.VMEM((NH, KC, NSUB, R, LANES), F32),
            pltpu.VMEM((trials, NSUB * R), jnp.int32),
            pltpu.VMEM((CD, QF * PER * R, NSUB * R), BF16),
            pltpu.VMEM((R, LANES), F32),
            pltpu.VMEM((lanes, R, LANES), F32),
            pltpu.VMEM((R, LANES), F32),
            pltpu.VMEM((lanes, R, LANES), F32),
            dma((2,)),
            dma((NH,)),
            dma((lanes, NH)),
            dma((lanes, NH)),
            dma((lanes,)),
            dma((lanes,)),
            dma((lanes,)),
            dma((lanes,)),
        ],
        compiler_params=pltpu.CompilerParams(
            collective_id=0, has_side_effects=True, vmem_limit_bytes=60 * 1024 * 1024
        ),
    )(spectra, rfi_flags, sub_delay, fine_delay)
    nw = widths.shape[0]
    return pl.pallas_call(
        functools.partial(detect_kernel, trials * lanes * samples),
        out_shape=jax.ShapeDtypeStruct((1, trials, nw), F32),
        in_specs=[vmem, vmem, pl.BlockSpec(memory_space=pltpu.SMEM), vmem],
        out_specs=vmem,
        scratch_shapes=[pltpu.VMEM((nw, trials, LANES), F32)],
    )(centered, total, widths, widths.reshape(1, nw))


def solution(mesh):
    in_specs = (P(None, "lane", None), P(None, "lane", None), P(None, "lane"), P("lane", None), P())
    out_specs = P("segment", "lane", None)
    return jax.shard_map(
        functools.partial(body, mesh.shape["lane"]),
        mesh=mesh, in_specs=in_specs, out_specs=out_specs, check_vma=False,
    )
```

```python
import functools

import jax
import jax.numpy as jnp
from jax import lax
from jax.experimental import pallas as pl
from jax.experimental.pallas import tpu as pltpu
from jax.sharding import PartitionSpec as P

D1 = 8
D2 = 32
WMAX = 64
LANES = 128

F32 = jnp.float32
BF16 = jnp.bfloat16


def iota(shape, axis):
    return lax.broadcasted_iota(jnp.int32, shape, axis)


def split(x):
    hi = x.astype(BF16)
    lo = (x - hi.astype(F32)).astype(BF16)
    return hi, lo


def dot(a, b):
    return lax.dot_general(a, b, (((1,), (0,)), ((), ())), preferred_element_type=F32)


def hot(mask):
    return jnp.where(mask, 1.0, 0.0).astype(BF16)


def shift_lanes(x, by):
    if by == 0:
        return x
    rolled = pltpu.roll(x, LANES - by, 1)
    return jnp.where(iota(x.shape, 1) < LANES - by, rolled, 0.0)


def shift_samples(x, by):
    n, R, L = x.shape
    if by % R == 0:
        return pltpu.roll(x.reshape(n * R, L), L - by // R, 1).reshape(n, R, L)
    y = pltpu.roll(x, R - by, 1)
    y1 = pltpu.roll(y.reshape(n * R, L), L - 1, 1).reshape(n, R, L)
    return jnp.where(iota((1, R, L), 1) >= R - by, y1, y)


def boxcars(x, widths_ref):
    n, R, L = x.shape
    upper_tri = hot(iota((L, L), 0) < iota((L, L), 1))
    flat = x.reshape(n * R, L)
    hi = flat.astype(BF16)
    rest = flat - hi.astype(F32)
    mid = rest.astype(BF16)
    lo = (rest - mid.astype(F32)).astype(BF16)
    before = dot(hi, upper_tri) + dot(mid, upper_tri) + dot(lo, upper_tri)
    before = jnp.sum(before.reshape(n, R, L), axis=1, keepdims=True)
    sub = iota((1, R, L), 1)
    pos = R * iota((1, R, L), 2) + sub
    run = x
    hop = 1
    while hop < R:
        run = run + jnp.where(sub >= hop, pltpu.roll(run, hop, 1), 0.0)
        hop *= 2
    prefix = before + run - x
    whole = jnp.sum(jnp.sum(x, axis=1, keepdims=True), axis=2, keepdims=True)
    out = jnp.zeros((n, LANES), F32)
    for wi in range(widths_ref.shape[0]):
        w = jnp.full((1, R, L), widths_ref[wi], jnp.int32)
        y = prefix
        by = 1
        while by <= WMAX:
            y = jnp.where((w & by) != 0, shift_samples(y, by), y)
            by *= 2
        y = jnp.where(pos + w >= R * L, whole, y)
        top = jnp.max(jnp.max(y - prefix, axis=1), axis=1, keepdims=True)
        out = jnp.where(iota((n, LANES), 1) == wi, top, out)
    return out


def search_kernel(
    cfg,
    spectra,
    flags,
    sub_delay,
    fine_delay,
    widths_ref,
    tops_ref,
    sigma_ref,
    power,
    flag_rows,
    tops,
    normed,
    perm,
    kept_all,
    delays2,
    wc,
    xs,
    out_blocks,
    incoming,
    fine_rep,
    wf,
    zmine,
    zall,
    smine,
    sall,
    in_sems,
    own_sems,
    send_sems,
    recv_sems,
    zsend,
    zrecv,
    ssend,
    srecv,
):
    lanes, R, NB, SUB, CD, NH, QC, QF, NSUB, PER = cfg
    KC = CD // NH
    samples = R * LANES
    rows = NB * SUB
    me = lax.axis_index("lane")
    batch = lax.axis_index("segment")

    row_step = min(64, rows)
    steps = rows // row_step

    def load(g):
        sl = pl.ds(pl.multiple_of(g * row_step, row_step), row_step)
        return pltpu.make_async_copy(spectra.at[batch, sl], power.at[sl], in_sems.at[g])

    load_flags = pltpu.make_async_copy(flags.at[batch], flag_rows, in_sems.at[steps])
    load_flags.start()
    for g in range(steps):
        load(g).start()

    def peer(step):
        return lax.rem(me + step, lanes)

    barrier = pltpu.get_barrier_semaphore()
    for step in range(1, lanes):
        pl.semaphore_signal(barrier, inc=1, device_id={"lane": peer(step)}, device_id_type=pl.DeviceIdType.MESH)

    pair = 2 * LANES
    chunk = pair // R
    per_lane_tile = LANES // chunk
    col = iota((pair, pair), 1)
    perm[...] = hot(iota((pair, pair), 0) == R * (col % chunk) + col // chunk)
    lane_row = iota((1, LANES), 1)

    load_flags.wait()
    blocks = flag_rows.shape[0]
    width = samples // blocks
    kept_all[...] = 1.0 - flag_rows[...].astype(F32).T

    def clean(g, _):
        sl = pl.ds(pl.multiple_of(g * row_step, row_step), row_step)
        load(g).wait()
        kept = kept_all[sl, :]
        mask = jnp.concatenate(
            [jnp.broadcast_to(kept[:, n : n + 1], (row_step, width)) for n in range(blocks)], axis=1
        )
        x = power[sl, :]
        masked = mask * x
        centre = jnp.sum(masked, axis=1, keepdims=True) * (1.0 / samples)
        off = masked - centre
        spread = jnp.sum(off * off, axis=1, keepdims=True) * (1.0 / samples)
        out = mask * (x - centre) * lax.rsqrt(spread + 1e-05)
        hi, lo = split(out)
        both = jnp.concatenate([hi, lo], axis=0)
        pieces = []
        for p in range(samples // pair):
            o = dot(both[:, p * pair : (p + 1) * pair], perm[...])
            pieces.append(o[:row_step] + o[row_step:])
        for r in range(R):
            tile, at = r // per_lane_tile, r % per_lane_tile * chunk
            dest = None
            for p, o in enumerate(pieces):
                x = o[:, tile * LANES : (tile + 1) * LANES]
                move = (p * chunk - at) % LANES
                x = pltpu.roll(x, move, 1) if move else x
                dest = x if dest is None else jnp.where(lane_row >= p * chunk, x, dest)
            normed[sl, r * LANES : (r + 1) * LANES] = dest
        return _

    lax.fori_loop(0, steps, clean, 0)

    for r in range(R):
        zmine[r : r + 1, :] = jnp.sum(normed[:, r * LANES : (r + 1) * LANES], axis=0, keepdims=True)
    zall[me] = zmine[...]
    pl.semaphore_wait(barrier, lanes - 1)

    def z_copy(step):
        return pltpu.make_async_remote_copy(
            zmine, zall.at[me], zsend.at[step], zrecv.at[step],
            device_id={"lane": peer(step)}, device_id_type=pl.DeviceIdType.MESH,
        )

    for step in range(1, lanes):
        z_copy(step).start()

    per_tile = LANES // SUB
    for b in range(NB):
        block = sub_delay[:, b * SUB : (b + 1) * SUB]
        delays2[b] = jnp.concatenate([block] * per_tile, axis=1)

    def coarse_weights(b, _):
        d = delays2[b]
        d = jnp.broadcast_to(d[:, None, :], (lanes * CD, R, LANES)).reshape(lanes, NH, KC, R, LANES)
        for h in range(NH):
            part = d[:, h].reshape(lanes * KC, R, LANES)
            for q in range(QC):
                for lt in range(R * SUB // LANES):
                    lag = R * q + lt * per_tile + iota((R, LANES), 1) // SUB - iota((R, LANES), 0)
                    n = lanes * KC * R
                    wc[b, h, q * n : (q + 1) * n, lt * LANES : (lt + 1) * LANES] = hot(part == lag[None]).reshape(n, LANES)
        return _

    lax.fori_loop(0, NB, coarse_weights, 0)

    for step in range(1, lanes):
        z_copy(step).wait()
    zero = zall[0]
    for e in range(1, lanes):
        zero = zero + zall[e]
    zmean = zero * (1.0 / (lanes * rows))

    def prepare(b, _):
        sl = pl.ds(pl.multiple_of(b * SUB, SUB), SUB)
        for r in range(R):
            part = normed[sl, r * LANES : (r + 1) * LANES] - zmean[r : r + 1, :]
            hi, lo = split(part)
            xs[b, r * SUB : (r + 1) * SUB, :LANES] = hi
            xs[b, r * SUB : (r + 1) * SUB, LANES:] = lo
        return _

    lax.fori_loop(0, NB, prepare, 0)

    def block_copy(step, h):
        e = peer(step)
        return pltpu.make_async_remote_copy(
            out_blocks.at[h, e],
            incoming.at[h, :, pl.ds(me * NB, NB)],
            send_sems.at[step, h],
            recv_sems.at[step, h],
            device_id={"lane": e},
            device_id_type=pl.DeviceIdType.MESH,
        )

    def own_copy(h):
        return pltpu.make_async_copy(
            out_blocks.at[h, me], incoming.at[h, :, pl.ds(me * NB, NB)], own_sems.at[h]
        )

    for h in range(NH):

        def coarse(b, _):
            n = lanes * KC * R
            o = dot(wc[b, h], xs[b])
            o = o[:, :LANES] + o[:, LANES:]
            total = o[:n]
            for q in range(1, QC):
                total = total + shift_lanes(o[q * n : (q + 1) * n], q)
            out_blocks[h, :, :, b] = total.reshape(lanes, KC, R, LANES)
            return _

        lax.fori_loop(0, NB, coarse, 0)
        for step in range(1, lanes):
            block_copy(step, h).start()
        own_copy(h).start()

    cols = NSUB * R
    rep = hot(iota((NSUB, cols), 1) // R == iota((NSUB, cols), 0))
    fine_rep[...] = dot(fine_delay[...].astype(F32).T.astype(BF16), rep).astype(jnp.int32)

    def fine_weights(k, _):
        sl = pl.ds(pl.multiple_of(k * PER, PER), PER)
        for lt in range(cols // LANES):
            d = fine_rep[sl, lt * LANES : (lt + 1) * LANES]
            d = jnp.broadcast_to(d[:, None, :], (PER, R, LANES))
            for q in range(QF):
                lag = R * q + iota((R, LANES), 1) % R - iota((R, LANES), 0)
                n = PER * R
                wf[k, q * n : (q + 1) * n, lt * LANES : (lt + 1) * LANES] = hot(d == lag[None]).reshape(n, LANES)
        return _

    lax.fori_loop(0, CD, fine_weights, 0)

    smine[...] = jnp.zeros_like(smine)
    for h in range(NH):
        own_copy(h).wait()
        for step in range(1, lanes):
            block_copy(step, h).wait_recv()

        def fine(kl, _):
            k = h * KC + kl
            n = PER * R
            hi, lo = split(incoming[h, kl].reshape(NSUB * R, LANES))
            o = dot(wf[k], jnp.concatenate([hi, lo], axis=1))
            o = o[:, :LANES] + o[:, LANES:]
            total = o[:n]
            for q in range(1, QF):
                total = total + shift_lanes(o[q * n : (q + 1) * n], q)
            series = total.reshape(PER, R, LANES)
            mean = jnp.sum(jnp.sum(series, axis=1, keepdims=True), axis=2, keepdims=True) * (1.0 / samples)
            series = series - mean
            tops[pl.ds(pl.multiple_of(k * PER, PER), PER), :] = boxcars(series, widths_ref)
            smine[...] += jnp.sum(series * series, axis=0)
            return _

        lax.fori_loop(0, KC, fine, 0)

    sall[me] = smine[...]

    def s_copy(step):
        return pltpu.make_async_remote_copy(
            smine, sall.at[me], ssend.at[step], srecv.at[step],
            device_id={"lane": peer(step)}, device_id_type=pl.DeviceIdType.MESH,
        )

    for step in range(1, lanes):
        s_copy(step).start()
    for h in range(NH):
        for step in range(1, lanes):
            block_copy(step, h).wait_send()
    for step in range(1, lanes):
        s_copy(step).wait()
    total = sall[0]
    for e in range(1, lanes):
        total = total + sall[e]
    total = jnp.sum(jnp.sum(total, axis=0, keepdims=True), axis=1, keepdims=True)
    sigma = jnp.sqrt(total * (1.0 / (lanes * CD * PER * samples)) + 1e-06)
    tops_ref[...] = tops[...].T[: tops_ref.shape[0]]
    sigma_ref[...] = jnp.broadcast_to(sigma, sigma_ref.shape)


def body(lanes, spectra, rfi_flags, sub_delay, fine_delay, widths):
    batches, rows, samples = spectra.shape
    R = samples // LANES
    coarse = sub_delay.shape[0]
    trials, NSUB = fine_delay.shape
    SUB = rows * lanes // NSUB
    NB = rows // SUB
    CD = coarse // lanes
    PER = trials // CD
    NH = min(8, CD)
    KC = CD // NH
    QC = (R - 1 + D1 - 1) // R + 1
    QF = (R - 1 + D2 - 1) // R + 1
    cfg = (lanes, R, NB, SUB, CD, NH, QC, QF, NSUB, PER)
    any_spec = pl.BlockSpec(memory_space=pl.ANY)
    vmem = pl.BlockSpec(memory_space=pltpu.VMEM)
    dma = pltpu.SemaphoreType.DMA
    nw = widths.shape[0]
    tops, sigma = pl.pallas_call(
        functools.partial(search_kernel, cfg),
        out_shape=(
            jax.ShapeDtypeStruct((nw, trials), F32),
            jax.ShapeDtypeStruct((nw, trials), F32),
        ),
        in_specs=[any_spec, any_spec, vmem, vmem, pl.BlockSpec(memory_space=pltpu.SMEM)],
        out_specs=(vmem, vmem),
        scratch_shapes=[
            pltpu.VMEM((rows, samples), F32),
            pltpu.VMEM((rfi_flags.shape[2], rows), jnp.int32),
            pltpu.VMEM((trials, LANES), F32),
            pltpu.VMEM((rows, samples), F32),
            pltpu.VMEM((2 * LANES, 2 * LANES), BF16),
            pltpu.VMEM((rows, rfi_flags.shape[2]), F32),
            pltpu.VMEM((NB, coarse, LANES), jnp.int32),
            pltpu.VMEM((NB, NH, QC * lanes * KC * R, R * SUB), BF16),
            pltpu.VMEM((NB, R * SUB, 2 * LANES), BF16),
            pltpu.VMEM((NH, lanes, KC, NB, R, LANES), F32),
            pltpu.VMEM((NH, KC, NSUB, R, LANES), F32),
            pltpu.VMEM((trials, NSUB * R), jnp.int32),
            pltpu.VMEM((CD, QF * PER * R, NSUB * R), BF16),
            pltpu.VMEM((R, LANES), F32),
            pltpu.VMEM((lanes, R, LANES), F32),
            pltpu.VMEM((R, LANES), F32),
            pltpu.VMEM((lanes, R, LANES), F32),
            dma((rows // min(64, rows) + 1,)),
            dma((NH,)),
            dma((lanes, NH)),
            dma((lanes, NH)),
            dma((lanes,)),
            dma((lanes,)),
            dma((lanes,)),
            dma((lanes,)),
        ],
        compiler_params=pltpu.CompilerParams(
            collective_id=0, has_side_effects=True, vmem_limit_bytes=60 * 1024 * 1024
        ),
    )(spectra, rfi_flags.transpose(0, 2, 1), sub_delay, fine_delay.T, widths)
    peaks = tops / (sigma * jnp.sqrt(widths.astype(F32))[:, None])
    return peaks.T[None]


def solution(mesh):
    in_specs = (P(None, "lane", None), P(None, "lane", None), P(None, "lane"), P("lane", None), P())
    out_specs = P("segment", "lane", None)
    return jax.shard_map(
        functools.partial(body, mesh.shape["lane"]),
        mesh=mesh, in_specs=in_specs, out_specs=out_specs, check_vma=False,
    )
```

```python
import functools

import jax
import jax.numpy as jnp
from jax import lax
from jax.experimental import pallas as pl
from jax.experimental.pallas import tpu as pltpu
from jax.sharding import PartitionSpec as P

D1 = 8
D2 = 32
WMAX = 64
LANES = 128

F32 = jnp.float32
BF16 = jnp.bfloat16


def iota(shape, axis):
    return lax.broadcasted_iota(jnp.int32, shape, axis)


def split(x):
    hi = x.astype(BF16)
    lo = (x - hi.astype(F32)).astype(BF16)
    return hi, lo


def dot(a, b):
    return lax.dot_general(a, b, (((1,), (0,)), ((), ())), preferred_element_type=F32)


def hot(mask):
    return jnp.where(mask, 1.0, 0.0).astype(BF16)


def shift_lanes(x, by):
    if by == 0:
        return x
    rolled = pltpu.roll(x, LANES - by, 1)
    return jnp.where(iota(x.shape, 1) < LANES - by, rolled, 0.0)


def boxcars(x, widths_ref, shifted):
    n, R, L = x.shape
    upper_tri = hot(iota((L, L), 0) < iota((L, L), 1))
    flat = x.reshape(n * R, L)
    hi = flat.astype(BF16)
    rest = flat - hi.astype(F32)
    mid = rest.astype(BF16)
    lo = (rest - mid.astype(F32)).astype(BF16)
    before = dot(hi, upper_tri) + dot(mid, upper_tri) + dot(lo, upper_tri)
    before = jnp.sum(before.reshape(n, R, L), axis=1, keepdims=True)
    sub = iota((1, R, L), 1)
    pos = R * iota((1, R, L), 2) + sub
    run = x
    hop = 1
    while hop < R:
        run = run + jnp.where(sub >= hop, pltpu.roll(run, hop, 1), 0.0)
        hop *= 2
    prefix = before + run - x
    whole = jnp.sum(jnp.sum(x, axis=1, keepdims=True), axis=2, keepdims=True)
    out = jnp.zeros((n, LANES), F32)
    rows = prefix.reshape(n * R, L)
    for a in range(shifted.shape[0]):
        shifted[a] = pltpu.roll(rows, L - a, 1) if a else rows
    for wi in range(widths_ref.shape[0]):
        width = widths_ref[wi]
        a = lax.div(width, R)
        w = jnp.full((1, R, L), width, jnp.int32)
        b = w - jnp.full((1, R, L), a, jnp.int32) * R
        here = shifted[a].reshape(n, R, L)
        after = shifted[a + 1].reshape(n, R, L)
        y = jnp.where(sub >= b, here, after)
        by = 1
        while by < R:
            y = jnp.where((b & by) != 0, pltpu.roll(y, R - by, 1), y)
            by *= 2
        y = jnp.where(pos + w >= R * L, whole, y)
        top = jnp.max(jnp.max(y - prefix, axis=1), axis=1, keepdims=True)
        out = jnp.where(iota((n, LANES), 1) == wi, top, out)
    return out


def search_kernel(
    cfg,
    spectra,
    flags,
    sub_delay,
    fine_delay,
    widths_ref,
    tops_ref,
    sigma_ref,
    power,
    flag_rows,
    tops,
    shifted,
    normed,
    perm,
    kept_all,
    delays2,
    wc,
    xs,
    out_blocks,
    incoming,
    fine_rep,
    wf,
    zmine,
    zall,
    smine,
    sall,
    in_sems,
    own_sems,
    send_sems,
    recv_sems,
    zsend,
    zrecv,
    ssend,
    srecv,
):
    lanes, R, NB, SUB, CD, NH, QC, QF, NSUB, PER = cfg
    KC = CD // NH
    samples = R * LANES
    rows = NB * SUB
    me = lax.axis_index("lane")
    batch = lax.axis_index("segment")

    row_step = min(64, rows)
    steps = rows // row_step

    def load(g):
        sl = pl.ds(pl.multiple_of(g * row_step, row_step), row_step)
        return pltpu.make_async_copy(spectra.at[batch, sl], power.at[sl], in_sems.at[g])

    load_flags = pltpu.make_async_copy(flags.at[batch], flag_rows, in_sems.at[steps])
    load_flags.start()
    for g in range(steps):
        load(g).start()

    def peer(step):
        return lax.rem(me + step, lanes)

    barrier = pltpu.get_barrier_semaphore()
    for step in range(1, lanes):
        pl.semaphore_signal(barrier, inc=1, device_id={"lane": peer(step)}, device_id_type=pl.DeviceIdType.MESH)

    pair = 2 * LANES
    chunk = pair // R
    per_lane_tile = LANES // chunk
    col = iota((pair, pair), 1)
    perm[...] = hot(iota((pair, pair), 0) == R * (col % chunk) + col // chunk)
    lane_row = iota((1, LANES), 1)

    load_flags.wait()
    blocks = flag_rows.shape[0]
    width = samples // blocks
    kept_all[...] = 1.0 - flag_rows[...].astype(F32).T

    def clean(g, _):
        sl = pl.ds(pl.multiple_of(g * row_step, row_step), row_step)
        load(g).wait()
        kept = kept_all[sl, :]
        mask = jnp.concatenate(
            [jnp.broadcast_to(kept[:, n : n + 1], (row_step, width)) for n in range(blocks)], axis=1
        )
        x = power[sl, :]
        masked = mask * x
        centre = jnp.sum(masked, axis=1, keepdims=True) * (1.0 / samples)
        off = masked - centre
        spread = jnp.sum(off * off, axis=1, keepdims=True) * (1.0 / samples)
        out = mask * (x - centre) * lax.rsqrt(spread + 1e-05)
        hi, lo = split(out)
        both = jnp.concatenate([hi, lo], axis=0)
        pieces = []
        for p in range(samples // pair):
            o = dot(both[:, p * pair : (p + 1) * pair], perm[...])
            pieces.append(o[:row_step] + o[row_step:])
        for r in range(R):
            tile, at = r // per_lane_tile, r % per_lane_tile * chunk
            dest = None
            for p, o in enumerate(pieces):
                x = o[:, tile * LANES : (tile + 1) * LANES]
                move = (p * chunk - at) % LANES
                x = pltpu.roll(x, move, 1) if move else x
                dest = x if dest is None else jnp.where(lane_row >= p * chunk, x, dest)
            normed[sl, r * LANES : (r + 1) * LANES] = dest
        return _

    lax.fori_loop(0, steps, clean, 0)

    for r in range(R):
        zmine[r : r + 1, :] = jnp.sum(normed[:, r * LANES : (r + 1) * LANES], axis=0, keepdims=True)
    zall[me] = zmine[...]
    pl.semaphore_wait(barrier, lanes - 1)

    def z_copy(step):
        return pltpu.make_async_remote_copy(
            zmine, zall.at[me], zsend.at[step], zrecv.at[step],
            device_id={"lane": peer(step)}, device_id_type=pl.DeviceIdType.MESH,
        )

    for step in range(1, lanes):
        z_copy(step).start()

    per_tile = LANES // SUB
    for b in range(NB):
        block = sub_delay[:, b * SUB : (b + 1) * SUB]
        delays2[b] = jnp.concatenate([block] * per_tile, axis=1)

    def coarse_weights(b, _):
        d = delays2[b]
        d = jnp.broadcast_to(d[:, None, :], (lanes * CD, R, LANES)).reshape(lanes, NH, KC, R, LANES)
        for h in range(NH):
            part = d[:, h].reshape(lanes * KC, R, LANES)
            for q in range(QC):
                for lt in range(R * SUB // LANES):
                    lag = R * q + lt * per_tile + iota((R, LANES), 1) // SUB - iota((R, LANES), 0)
                    n = lanes * KC * R
                    wc[b, h, q * n : (q + 1) * n, lt * LANES : (lt + 1) * LANES] = hot(part == lag[None]).reshape(n, LANES)
        return _

    lax.fori_loop(0, NB, coarse_weights, 0)

    for step in range(1, lanes):
        z_copy(step).wait()
    zero = zall[0]
    for e in range(1, lanes):
        zero = zero + zall[e]
    zmean = zero * (1.0 / (lanes * rows))

    def prepare(b, _):
        sl = pl.ds(pl.multiple_of(b * SUB, SUB), SUB)
        for r in range(R):
            part = normed[sl, r * LANES : (r + 1) * LANES] - zmean[r : r + 1, :]
            hi, lo = split(part)
            xs[b, r * SUB : (r + 1) * SUB, :LANES] = hi
            xs[b, r * SUB : (r + 1) * SUB, LANES:] = lo
        return _

    lax.fori_loop(0, NB, prepare, 0)

    def block_copy(step, h):
        e = peer(step)
        return pltpu.make_async_remote_copy(
            out_blocks.at[h, e],
            incoming.at[h, :, pl.ds(me * NB, NB)],
            send_sems.at[step, h],
            recv_sems.at[step, h],
            device_id={"lane": e},
            device_id_type=pl.DeviceIdType.MESH,
        )

    def own_copy(h):
        return pltpu.make_async_copy(
            out_blocks.at[h, me], incoming.at[h, :, pl.ds(me * NB, NB)], own_sems.at[h]
        )

    for h in range(NH):

        def coarse(b, _):
            n = lanes * KC * R
            o = dot(wc[b, h], xs[b])
            o = o[:, :LANES] + o[:, LANES:]
            total = o[:n]
            for q in range(1, QC):
                total = total + shift_lanes(o[q * n : (q + 1) * n], q)
            out_blocks[h, :, :, b] = total.reshape(lanes, KC, R, LANES)
            return _

        lax.fori_loop(0, NB, coarse, 0)
        for step in range(1, lanes):
            block_copy(step, h).start()
        own_copy(h).start()

    cols = NSUB * R
    rep = hot(iota((NSUB, cols), 1) // R == iota((NSUB, cols), 0))
    fine_rep[...] = dot(fine_delay[...].astype(F32).T.astype(BF16), rep).astype(jnp.int32)

    def fine_weights(k, _):
        sl = pl.ds(pl.multiple_of(k * PER, PER), PER)
        for lt in range(cols // LANES):
            d = fine_rep[sl, lt * LANES : (lt + 1) * LANES]
            d = jnp.broadcast_to(d[:, None, :], (PER, R, LANES))
            for q in range(QF):
                lag = R * q + iota((R, LANES), 1) % R - iota((R, LANES), 0)
                n = PER * R
                wf[k, q * n : (q + 1) * n, lt * LANES : (lt + 1) * LANES] = hot(d == lag[None]).reshape(n, LANES)
        return _

    lax.fori_loop(0, CD, fine_weights, 0)

    smine[...] = jnp.zeros_like(smine)
    for h in range(NH):
        own_copy(h).wait()
        for step in range(1, lanes):
            block_copy(step, h).wait_recv()

        def fine(kl, _):
            k = h * KC + kl
            n = PER * R
            hi, lo = split(incoming[h, kl].reshape(NSUB * R, LANES))
            o = dot(wf[k], jnp.concatenate([hi, lo], axis=1))
            o = o[:, :LANES] + o[:, LANES:]
            total = o[:n]
            for q in range(1, QF):
                total = total + shift_lanes(o[q * n : (q + 1) * n], q)
            series = total.reshape(PER, R, LANES)
            mean = jnp.sum(jnp.sum(series, axis=1, keepdims=True), axis=2, keepdims=True) * (1.0 / samples)
            series = series - mean
            tops[pl.ds(pl.multiple_of(k * PER, PER), PER), :] = boxcars(series, widths_ref, shifted)
            smine[...] += jnp.sum(series * series, axis=0)
            return _

        lax.fori_loop(0, KC, fine, 0)

    sall[me] = smine[...]

    def s_copy(step):
        return pltpu.make_async_remote_copy(
            smine, sall.at[me], ssend.at[step], srecv.at[step],
            device_id={"lane": peer(step)}, device_id_type=pl.DeviceIdType.MESH,
        )

    for step in range(1, lanes):
        s_copy(step).start()
    for h in range(NH):
        for step in range(1, lanes):
            block_copy(step, h).wait_send()
    for step in range(1, lanes):
        s_copy(step).wait()
    total = sall[0]
    for e in range(1, lanes):
        total = total + sall[e]
    total = jnp.sum(jnp.sum(total, axis=0, keepdims=True), axis=1, keepdims=True)
    sigma = jnp.sqrt(total * (1.0 / (lanes * CD * PER * samples)) + 1e-06)
    tops_ref[...] = tops[...].T[: tops_ref.shape[0]]
    sigma_ref[...] = jnp.broadcast_to(sigma, sigma_ref.shape)


def body(lanes, spectra, rfi_flags, sub_delay, fine_delay, widths):
    batches, rows, samples = spectra.shape
    R = samples // LANES
    coarse = sub_delay.shape[0]
    trials, NSUB = fine_delay.shape
    SUB = rows * lanes // NSUB
    NB = rows // SUB
    CD = coarse // lanes
    PER = trials // CD
    NH = min(8, CD)
    KC = CD // NH
    QC = (R - 1 + D1 - 1) // R + 1
    QF = (R - 1 + D2 - 1) // R + 1
    cfg = (lanes, R, NB, SUB, CD, NH, QC, QF, NSUB, PER)
    any_spec = pl.BlockSpec(memory_space=pl.ANY)
    vmem = pl.BlockSpec(memory_space=pltpu.VMEM)
    dma = pltpu.SemaphoreType.DMA
    nw = widths.shape[0]
    tops, sigma = pl.pallas_call(
        functools.partial(search_kernel, cfg),
        out_shape=(
            jax.ShapeDtypeStruct((nw, trials), F32),
            jax.ShapeDtypeStruct((nw, trials), F32),
        ),
        in_specs=[any_spec, any_spec, vmem, vmem, pl.BlockSpec(memory_space=pltpu.SMEM)],
        out_specs=(vmem, vmem),
        scratch_shapes=[
            pltpu.VMEM((rows, samples), F32),
            pltpu.VMEM((rfi_flags.shape[2], rows), jnp.int32),
            pltpu.VMEM((trials, LANES), F32),
            pltpu.VMEM((WMAX // R + 2, PER * R, LANES), F32),
            pltpu.VMEM((rows, samples), F32),
            pltpu.VMEM((2 * LANES, 2 * LANES), BF16),
            pltpu.VMEM((rows, rfi_flags.shape[2]), F32),
            pltpu.VMEM((NB, coarse, LANES), jnp.int32),
            pltpu.VMEM((NB, NH, QC * lanes * KC * R, R * SUB), BF16),
            pltpu.VMEM((NB, R * SUB, 2 * LANES), BF16),
            pltpu.VMEM((NH, lanes, KC, NB, R, LANES), F32),
            pltpu.VMEM((NH, KC, NSUB, R, LANES), F32),
            pltpu.VMEM((trials, NSUB * R), jnp.int32),
            pltpu.VMEM((CD, QF * PER * R, NSUB * R), BF16),
            pltpu.VMEM((R, LANES), F32),
            pltpu.VMEM((lanes, R, LANES), F32),
            pltpu.VMEM((R, LANES), F32),
            pltpu.VMEM((lanes, R, LANES), F32),
            dma((rows // min(64, rows) + 1,)),
            dma((NH,)),
            dma((lanes, NH)),
            dma((lanes, NH)),
            dma((lanes,)),
            dma((lanes,)),
            dma((lanes,)),
            dma((lanes,)),
        ],
        compiler_params=pltpu.CompilerParams(
            collective_id=0, has_side_effects=True, vmem_limit_bytes=60 * 1024 * 1024
        ),
    )(spectra, rfi_flags.transpose(0, 2, 1), sub_delay, fine_delay.T, widths)
    peaks = tops / (sigma * jnp.sqrt(widths.astype(F32))[:, None])
    return peaks.T[None]


def solution(mesh):
    in_specs = (P(None, "lane", None), P(None, "lane", None), P(None, "lane"), P("lane", None), P())
    out_specs = P("segment", "lane", None)
    return jax.shard_map(
        functools.partial(body, mesh.shape["lane"]),
        mesh=mesh, in_specs=in_specs, out_specs=out_specs, check_vma=False,
    )
```

```python
import functools

import jax
import jax.numpy as jnp
from jax import lax
from jax.experimental import pallas as pl
from jax.experimental.pallas import tpu as pltpu
from jax.sharding import PartitionSpec as P

D1 = 8
D2 = 32
WMAX = 64
LANES = 128

F32 = jnp.float32
BF16 = jnp.bfloat16


def iota(shape, axis):
    return lax.broadcasted_iota(jnp.int32, shape, axis)


def split(x):
    hi = x.astype(BF16)
    lo = (x - hi.astype(F32)).astype(BF16)
    return hi, lo


def dot(a, b):
    return lax.dot_general(a, b, (((1,), (0,)), ((), ())), preferred_element_type=F32)


def hot(mask):
    return jnp.where(mask, 1.0, 0.0).astype(BF16)


def shift_lanes(x, by):
    if by == 0:
        return x
    rolled = pltpu.roll(x, LANES - by, 1)
    return jnp.where(iota(x.shape, 1) < LANES - by, rolled, 0.0)


def boxcars(x, widths_ref, shifted):
    n, R, L = x.shape
    upper_tri = hot(iota((L, L), 0) < iota((L, L), 1))
    flat = x.reshape(n * R, L)
    hi = flat.astype(BF16)
    rest = flat - hi.astype(F32)
    mid = rest.astype(BF16)
    lo = (rest - mid.astype(F32)).astype(BF16)
    before = dot(hi, upper_tri) + dot(mid, upper_tri) + dot(lo, upper_tri)
    before = jnp.sum(before.reshape(n, R, L), axis=1, keepdims=True)
    sub = iota((1, R, L), 1)
    pos = R * iota((1, R, L), 2) + sub
    run = x
    hop = 1
    while hop < R:
        run = run + jnp.where(sub >= hop, pltpu.roll(run, hop, 1), 0.0)
        hop *= 2
    prefix = before + run - x
    whole = jnp.sum(jnp.sum(x, axis=1, keepdims=True), axis=2, keepdims=True)
    out = jnp.zeros((n, LANES), F32)
    rows = prefix.reshape(n * R, L)
    for a in range(shifted.shape[0]):
        shifted[a] = pltpu.roll(rows, L - a, 1) if a else rows
    for wi in range(widths_ref.shape[0]):
        width = widths_ref[wi]
        a = lax.div(width, R)
        w = jnp.full((1, R, L), width, jnp.int32)
        b = w - jnp.full((1, R, L), a, jnp.int32) * R
        here = shifted[a].reshape(n, R, L)
        after = shifted[a + 1].reshape(n, R, L)
        y = jnp.where(sub >= b, here, after)
        by = 1
        while by < R:
            y = jnp.where((b & by) != 0, pltpu.roll(y, R - by, 1), y)
            by *= 2
        y = jnp.where(pos + w >= R * L, whole, y)
        top = jnp.max(jnp.max(y - prefix, axis=1), axis=1, keepdims=True)
        out = jnp.where(iota((n, LANES), 1) == wi, top, out)
    return out


def search_kernel(
    cfg,
    spectra,
    flags,
    sub_delay,
    fine_delay,
    widths_ref,
    tops_ref,
    sigma_ref,
    power,
    flag_rows,
    tops,
    shifted,
    normed,
    perm,
    kept_all,
    delays2,
    wc,
    xs,
    out_blocks,
    incoming,
    fine_rep,
    wf,
    zmine,
    zall,
    smine,
    sall,
    in_sems,
    own_sems,
    send_sems,
    recv_sems,
    zsend,
    zrecv,
    ssend,
    srecv,
):
    lanes, R, NB, SUB, CD, NH, QC, QF, NSUB, PER = cfg
    KC = CD // NH
    samples = R * LANES
    rows = NB * SUB
    me = lax.axis_index("lane")
    batch = lax.axis_index("segment")

    row_step = min(64, rows)
    steps = rows // row_step

    def load(g):
        sl = pl.ds(pl.multiple_of(g * row_step, row_step), row_step)
        return pltpu.make_async_copy(spectra.at[batch, sl], power.at[sl], in_sems.at[g])

    load_flags = pltpu.make_async_copy(flags.at[batch], flag_rows, in_sems.at[steps])
    load_flags.start()
    for g in range(steps):
        load(g).start()

    def peer(step):
        return lax.rem(me + step, lanes)

    barrier = pltpu.get_barrier_semaphore()
    for step in range(1, lanes):
        pl.semaphore_signal(barrier, inc=1, device_id={"lane": peer(step)}, device_id_type=pl.DeviceIdType.MESH)

    pair = 2 * LANES
    chunk = pair // R
    per_lane_tile = LANES // chunk
    col = iota((pair, pair), 1)
    perm[...] = hot(iota((pair, pair), 0) == R * (col % chunk) + col // chunk)
    lane_row = iota((1, LANES), 1)

    load_flags.wait()
    blocks = flag_rows.shape[0]
    width = samples // blocks
    kept_all[...] = 1.0 - flag_rows[...].astype(F32).T

    def clean(g, _):
        sl = pl.ds(pl.multiple_of(g * row_step, row_step), row_step)
        load(g).wait()
        kept = kept_all[sl, :]
        mask = jnp.concatenate(
            [jnp.broadcast_to(kept[:, n : n + 1], (row_step, width)) for n in range(blocks)], axis=1
        )
        x = power[sl, :]
        masked = mask * x
        centre = jnp.sum(masked, axis=1, keepdims=True) * (1.0 / samples)
        off = masked - centre
        spread = jnp.sum(off * off, axis=1, keepdims=True) * (1.0 / samples)
        out = mask * (x - centre) * lax.rsqrt(spread + 1e-05)
        hi, lo = split(out)
        both = jnp.concatenate([hi, lo], axis=0)
        pieces = []
        for p in range(samples // pair):
            o = dot(both[:, p * pair : (p + 1) * pair], perm[...])
            pieces.append(o[:row_step] + o[row_step:])
        for r in range(R):
            tile, at = r // per_lane_tile, r % per_lane_tile * chunk
            dest = None
            for p, o in enumerate(pieces):
                x = o[:, tile * LANES : (tile + 1) * LANES]
                move = (p * chunk - at) % LANES
                x = pltpu.roll(x, move, 1) if move else x
                dest = x if dest is None else jnp.where(lane_row >= p * chunk, x, dest)
            normed[sl, r * LANES : (r + 1) * LANES] = dest
        return _

    lax.fori_loop(0, steps, clean, 0)

    for r in range(R):
        zmine[r : r + 1, :] = jnp.sum(normed[:, r * LANES : (r + 1) * LANES], axis=0, keepdims=True)
    zall[me] = zmine[...]
    pl.semaphore_wait(barrier, lanes - 1)

    def z_copy(step):
        return pltpu.make_async_remote_copy(
            zmine, zall.at[me], zsend.at[step], zrecv.at[step],
            device_id={"lane": peer(step)}, device_id_type=pl.DeviceIdType.MESH,
        )

    for step in range(1, lanes):
        z_copy(step).start()

    per_tile = LANES // SUB
    for b in range(NB):
        block = sub_delay[:, b * SUB : (b + 1) * SUB]
        delays2[b] = jnp.concatenate([block] * per_tile, axis=1)

    def coarse_weights(b, _):
        d = delays2[b]
        d = jnp.broadcast_to(d[:, None, :], (lanes * CD, R, LANES)).reshape(lanes, NH, KC, R, LANES)
        for h in range(NH):
            part = d[:, h].reshape(lanes * KC, R, LANES)
            for q in range(QC):
                for lt in range(R * SUB // LANES):
                    lag = R * q + lt * per_tile + iota((R, LANES), 1) // SUB - iota((R, LANES), 0)
                    n = lanes * KC * R
                    wc[b, h, q * n : (q + 1) * n, lt * LANES : (lt + 1) * LANES] = hot(part == lag[None]).reshape(n, LANES)
        return _

    lax.fori_loop(0, NB, coarse_weights, 0)

    for step in range(1, lanes):
        z_copy(step).wait()
    zero = zall[0]
    for e in range(1, lanes):
        zero = zero + zall[e]
    zmean = zero * (1.0 / (lanes * rows))

    def prepare(b, _):
        sl = pl.ds(pl.multiple_of(b * SUB, SUB), SUB)
        for r in range(R):
            part = normed[sl, r * LANES : (r + 1) * LANES] - zmean[r : r + 1, :]
            hi, lo = split(part)
            xs[b, r * SUB : (r + 1) * SUB, :LANES] = hi
            xs[b, r * SUB : (r + 1) * SUB, LANES:] = lo
        return _

    lax.fori_loop(0, NB, prepare, 0)

    def block_copy(step, h):
        e = peer(step)
        return pltpu.make_async_remote_copy(
            out_blocks.at[h, e],
            incoming.at[h, :, pl.ds(me * NB, NB)],
            send_sems.at[step, h],
            recv_sems.at[step, h],
            device_id={"lane": e},
            device_id_type=pl.DeviceIdType.MESH,
        )

    def own_copy(h):
        return pltpu.make_async_copy(
            out_blocks.at[h, me], incoming.at[h, :, pl.ds(me * NB, NB)], own_sems.at[h]
        )

    for h in range(NH):

        def coarse(b, _):
            n = lanes * KC * R
            o = dot(wc[b, h], xs[b])
            o = o[:, :LANES] + o[:, LANES:]
            total = o[:n]
            for q in range(1, QC):
                total = total + shift_lanes(o[q * n : (q + 1) * n], q)
            out_blocks[h, :, :, b] = total.reshape(lanes, KC, R, LANES)
            return _

        lax.fori_loop(0, NB, coarse, 0)
        for step in range(1, lanes):
            block_copy(step, h).start()
        own_copy(h).start()

    cols = NSUB * R
    rep = hot(iota((NSUB, cols), 1) // R == iota((NSUB, cols), 0))
    fine_rep[...] = dot(fine_delay[...].astype(F32).T.astype(BF16), rep).astype(jnp.int32)

    def fine_weights(k, _):
        sl = pl.ds(pl.multiple_of(k * PER, PER), PER)
        for lt in range(cols // LANES):
            d = fine_rep[sl, lt * LANES : (lt + 1) * LANES]
            d = jnp.broadcast_to(d[:, None, :], (PER, R, LANES))
            for q in range(QF):
                lag = R * q + iota((R, LANES), 1) % R - iota((R, LANES), 0)
                n = PER * R
                wf[k, q * n : (q + 1) * n, lt * LANES : (lt + 1) * LANES] = hot(d == lag[None]).reshape(n, LANES)
        return _

    lax.fori_loop(0, CD, fine_weights, 0)

    smine[...] = jnp.zeros_like(smine)
    for h in range(NH):
        own_copy(h).wait()
        for step in range(1, lanes):
            block_copy(step, h).wait_recv()

        def fine(kl, _):
            k = h * KC + kl
            n = PER * R
            hi, lo = split(incoming[h, kl].reshape(NSUB * R, LANES))
            o = dot(wf[k], jnp.concatenate([hi, lo], axis=1))
            o = o[:, :LANES] + o[:, LANES:]
            total = o[:n]
            for q in range(1, QF):
                total = total + shift_lanes(o[q * n : (q + 1) * n], q)
            series = total.reshape(PER, R, LANES)
            mean = jnp.sum(jnp.sum(series, axis=1, keepdims=True), axis=2, keepdims=True) * (1.0 / samples)
            series = series - mean
            tops[pl.ds(pl.multiple_of(k * PER, PER), PER), :] = boxcars(series, widths_ref, shifted)
            smine[...] += jnp.sum(series * series, axis=0)
            return _

        lax.fori_loop(0, KC, fine, 0)

    sall[me] = smine[...]

    def s_copy(step):
        return pltpu.make_async_remote_copy(
            smine, sall.at[me], ssend.at[step], srecv.at[step],
            device_id={"lane": peer(step)}, device_id_type=pl.DeviceIdType.MESH,
        )

    for step in range(1, lanes):
        s_copy(step).start()
    for h in range(NH):
        for step in range(1, lanes):
            block_copy(step, h).wait_send()
    for step in range(1, lanes):
        s_copy(step).wait()
    total = sall[0]
    for e in range(1, lanes):
        total = total + sall[e]
    total = jnp.sum(jnp.sum(total, axis=0, keepdims=True), axis=1, keepdims=True)
    sigma = jnp.sqrt(total * (1.0 / (lanes * CD * PER * samples)) + 1e-06)
    tops_ref[...] = tops[...].T[: tops_ref.shape[0]]
    for wi in range(sigma_ref.shape[0]):
        w = jnp.full((1, sigma_ref.shape[1]), widths_ref[wi], jnp.int32).astype(F32)
        sigma_ref[wi : wi + 1, :] = sigma * jnp.sqrt(w)


def body(lanes, spectra, rfi_flags, sub_delay, fine_delay, widths):
    batches, rows, samples = spectra.shape
    R = samples // LANES
    coarse = sub_delay.shape[0]
    trials, NSUB = fine_delay.shape
    SUB = rows * lanes // NSUB
    NB = rows // SUB
    CD = coarse // lanes
    PER = trials // CD
    NH = min(8, CD)
    KC = CD // NH
    QC = (R - 1 + D1 - 1) // R + 1
    QF = (R - 1 + D2 - 1) // R + 1
    cfg = (lanes, R, NB, SUB, CD, NH, QC, QF, NSUB, PER)
    any_spec = pl.BlockSpec(memory_space=pl.ANY)
    vmem = pl.BlockSpec(memory_space=pltpu.VMEM)
    dma = pltpu.SemaphoreType.DMA
    nw = widths.shape[0]
    tops, sigma = pl.pallas_call(
        functools.partial(search_kernel, cfg),
        out_shape=(
            jax.ShapeDtypeStruct((nw, trials), F32),
            jax.ShapeDtypeStruct((nw, trials), F32),
        ),
        in_specs=[any_spec, any_spec, vmem, vmem, pl.BlockSpec(memory_space=pltpu.SMEM)],
        out_specs=(vmem, vmem),
        scratch_shapes=[
            pltpu.VMEM((rows, samples), F32),
            pltpu.VMEM((rfi_flags.shape[2], rows), jnp.int32),
            pltpu.VMEM((trials, LANES), F32),
            pltpu.VMEM((WMAX // R + 2, PER * R, LANES), F32),
            pltpu.VMEM((rows, samples), F32),
            pltpu.VMEM((2 * LANES, 2 * LANES), BF16),
            pltpu.VMEM((rows, rfi_flags.shape[2]), F32),
            pltpu.VMEM((NB, coarse, LANES), jnp.int32),
            pltpu.VMEM((NB, NH, QC * lanes * KC * R, R * SUB), BF16),
            pltpu.VMEM((NB, R * SUB, 2 * LANES), BF16),
            pltpu.VMEM((NH, lanes, KC, NB, R, LANES), F32),
            pltpu.VMEM((NH, KC, NSUB, R, LANES), F32),
            pltpu.VMEM((trials, NSUB * R), jnp.int32),
            pltpu.VMEM((CD, QF * PER * R, NSUB * R), BF16),
            pltpu.VMEM((R, LANES), F32),
            pltpu.VMEM((lanes, R, LANES), F32),
            pltpu.VMEM((R, LANES), F32),
            pltpu.VMEM((lanes, R, LANES), F32),
            dma((rows // min(64, rows) + 1,)),
            dma((NH,)),
            dma((lanes, NH)),
            dma((lanes, NH)),
            dma((lanes,)),
            dma((lanes,)),
            dma((lanes,)),
            dma((lanes,)),
        ],
        compiler_params=pltpu.CompilerParams(
            collective_id=0, has_side_effects=True, vmem_limit_bytes=60 * 1024 * 1024
        ),
    )(spectra, rfi_flags.transpose(0, 2, 1), sub_delay, fine_delay.T, widths)
    peaks = tops / sigma
    return peaks.T[None]


def solution(mesh):
    in_specs = (P(None, "lane", None), P(None, "lane", None), P(None, "lane"), P("lane", None), P())
    out_specs = P("segment", "lane", None)
    return jax.shard_map(
        functools.partial(body, mesh.shape["lane"]),
        mesh=mesh, in_specs=in_specs, out_specs=out_specs, check_vma=False,
    )
```
